128 devices in a mesh: au: 16 (over x, z_lo, core), ia: 8 (over y, z_hi).
Axes of the slice: x: 4, y: 4, z: 4 (z_hi: 2, z_lo: 2; z = z_hi * 2 + z_lo), core: 2. Of those that a mesh axis runs over, the one named last changes fastest.
Arguments:
- users: float32 [262144, 256], P(('au', 'ia')), may hold values from -6 to 6
- items: float32 [32768, 256], P(('au', 'ia')), may hold values from -6 to 6
- accum: float32 [32768, 256], P(('au', 'ia')), may hold values from 0.1 to 4
- ratings: bfloat16 [16, 8, 2, 16, 128, 128], P('au', 'ia'), may hold values from -6 to 6
- block_users: int32 [16, 8, 2, 16], P(None, 'ia'), may hold values from 0 to 15, as said below
- block_items: int32 [16, 8, 2, 16], P(None, 'ia'), may hold values from 0 to 1, as said below
- block_counts: int32 [16, 8, 2], P(None, 'ia'), may hold values from 2 to 16, as said below
Outputs:
- new_users: float32 [262144, 256], P(('au', 'ia'))
- new_items: float32 [32768, 256], P(('au', 'ia'))
- new_accum: float32 [32768, 256], P(('au', 'ia'))
The draws below stay inside these ranges and needn't reach their ends.
Inputs may be any that keep to these rules, and one draw needn't show every extreme that they name: In each pair and stratum the 16 slots name distinct (user block, item block) pairs, block_users with block_items. `block_items`: see block_users. Only the first block_counts slots of a pair and stratum are observed; in every stratum some pair has all 16 slots observed.
All inputs are finite; a program needn't handle non-finite values.
Results may differ from the reference program's by a relative error of at most 0.008.
Values may be sent and summed in bfloat16 or wider, within the bound.
No kernel may reach another device: no remote copies, remote signals or barrier semaphores. Data moves between devices by JAX's collectives and lax.ppermute only.
A program may use at most 64 MiB of HBM per device.

```python
import math
import jax
import jax.numpy as jnp
from jax import lax

K = 256
BLOCK = 128
UB_DEV = 16
IB_DEV = 2
STRATA = 2
STEPS = 2
NB = 16
USERS = 262144
ITEMS = 32768
N_AU = 16
N_IA = 8


def pair_codes(key):
    count_all = N_AU * N_IA * STRATA
    subkeys = jax.random.split(jax.random.fold_in(key, 11), count_all)
    shuffled = jax.vmap(lambda subkey: jax.random.permutation(subkey, UB_DEV * IB_DEV))(subkeys)
    return shuffled[:, :NB].reshape(N_AU, N_IA, STRATA, NB).astype(jnp.int32)


def draw_block_users(key, part):
    return pair_codes(key) // IB_DEV


def draw_block_items(key, part):
    return pair_codes(key) % IB_DEV


def draw_block_counts(key, part):
    divisor = jax.random.randint(jax.random.fold_in(key, 3), (N_AU * N_IA, STRATA), 1, 7)
    counts = jnp.maximum(NB // divisor, 1)
    heaviest = jax.random.randint(jax.random.fold_in(key, 5), (STRATA,), 0, N_AU * N_IA)
    chosen = jnp.arange(N_AU * N_IA)[:, None] == heaviest[None, :]
    return jnp.where(chosen, NB, counts).reshape(N_AU, N_IA, STRATA).astype(jnp.int32)


def steps_of(stream_key, shape, pieces, smallest, high):
    gain = 1.0
    for axis_at, blocks in pieces:
        steps = jax.random.uniform(jax.random.fold_in(jax.random.fold_in(stream_key, 6), axis_at), (blocks,), jnp.float32, smallest / len(pieces), high / len(pieces))
        gain = gain * jnp.repeat(jnp.exp(steps), shape[axis_at] // blocks).reshape((-1,) + (1,) * (len(shape) - 1 - axis_at))
    return gain


def bell_draw(stream_key, extent, scale, bound, pieces=(), kind=jnp.bfloat16):
    result = scale * jax.random.normal(stream_key, extent, jnp.float32)
    if pieces:
        result = result * steps_of(stream_key, extent, pieces, -0.22, 0.18)
    return jnp.clip(result, -bound, bound).astype(kind)


def setup_inputs(seed: int = 0) -> dict:
    splits = jax.random.split(jax.random.key(seed), 8)
    users = bell_draw(splits[0], (USERS, K), 1.0, 6.0, ((0, 128),), jnp.float32)
    items = bell_draw(splits[1], (ITEMS, K), 1.0, 6.0, ((0, 128),), jnp.float32)
    accum = jnp.clip(jnp.exp(math.log(4.0) - 3.6888794 * jax.random.uniform(splits[2], (ITEMS, K), jnp.float32) ** steps_of(splits[2], (ITEMS, K), ((0, 128),), -0.2, 0.2)), 0.1, 4.0)
    ratings = bell_draw(splits[3], (N_AU, N_IA, STRATA, NB, BLOCK, BLOCK), 1.0, 6.0, ((0, 16), (1, 8)))
    block_users = draw_block_users(jax.random.fold_in(splits[7], 71), 0)
    block_items = draw_block_items(jax.random.fold_in(splits[7], 71), 0)
    block_counts = draw_block_counts(jax.random.fold_in(splits[7], 71), 0)
    return dict(users=users, items=items, accum=accum, ratings=ratings, block_users=block_users, block_items=block_items, block_counts=block_counts)


rate_users = 0.1
rate_items = 0.1
weight_decay = 0.02
adagrad_eps = 1e-08

def hold_round(values):
    return lax.optimization_barrier(values.astype(jnp.bfloat16)).astype(jnp.float32)

def stratum_update(packed):
    user_slab, item_slab, accum_slab, rating_set, user_ids, item_ids, live_count = packed
    inv_root = 1.0 / math.sqrt(user_slab.shape[-1])
    slot_ids = jnp.arange(rating_set.shape[0], dtype=jnp.int32)
    live_mask = (slot_ids < live_count)[:, None, None]
    pick_users = (user_ids[:, None] == jnp.arange(user_slab.shape[0], dtype=jnp.int32)[None, :]).astype(jnp.float32)
    pick_items = (item_ids[:, None] == jnp.arange(item_slab.shape[0], dtype=jnp.int32)[None, :]).astype(jnp.float32)
    highest = lax.Precision.HIGHEST
    for repeat in range(STEPS):
        user_rows = hold_round(user_slab)[user_ids]
        item_rows = hold_round(item_slab)[item_ids]
        predicted = jnp.einsum('nrk,nck->nrc', user_rows, item_rows, precision=highest)
        residual = hold_round(jnp.where(live_mask, rating_set.astype(jnp.float32) - inv_root * predicted, 0.0))
        user_part = jnp.einsum('nrc,nck->nrk', residual, item_rows, precision=highest)
        item_part = jnp.einsum('nrc,nrk->nck', residual, user_rows, precision=highest)
        user_sum = jnp.einsum('nu,nrk->urk', pick_users, user_part, precision=highest)
        item_sum = jnp.einsum('ni,nck->ick', pick_items, item_part, precision=highest)
        user_grad = weight_decay * user_slab - inv_root * user_sum
        item_grad = weight_decay * item_slab - inv_root * item_sum
        user_slab = user_slab - rate_users * user_grad
        accum_slab = accum_slab + item_grad * item_grad
        item_slab = item_slab - rate_items * item_grad / jnp.sqrt(accum_slab + adagrad_eps)
    return (user_slab, item_slab, accum_slab)

def reference(users, items, accum, ratings, block_users, block_items, block_counts):
    rank_width = users.shape[-1]
    block_size = ratings.shape[-1]
    device_count = N_AU * N_IA
    user_grid = users.reshape(N_AU, N_IA, UB_DEV, block_size, rank_width)
    item_grid = items.reshape(N_AU, N_IA, IB_DEV, block_size, rank_width)
    accum_grid = accum.reshape(N_AU, N_IA, IB_DEV, block_size, rank_width)
    for stratum in range(STRATA):
        user_now = jnp.roll(user_grid, stratum, axis=0).reshape(device_count, UB_DEV, block_size, rank_width)
        item_now = jnp.roll(item_grid, stratum, axis=1).reshape(device_count, IB_DEV, block_size, rank_width)
        accum_now = jnp.roll(accum_grid, stratum, axis=1).reshape(device_count, IB_DEV, block_size, rank_width)
        rating_now = ratings[:, :, stratum].reshape(device_count, NB, block_size, block_size)
        user_ids_now = block_users[:, :, stratum].reshape(device_count, NB)
        item_ids_now = block_items[:, :, stratum].reshape(device_count, NB)
        counts_now = block_counts[:, :, stratum].reshape(device_count)
        user_new, item_new, accum_new = lax.map(stratum_update, (user_now, item_now, accum_now, rating_now, user_ids_now, item_ids_now, counts_now))
        user_grid = jnp.roll(user_new.reshape(N_AU, N_IA, UB_DEV, block_size, rank_width), -stratum, axis=0)
        item_grid = jnp.roll(item_new.reshape(N_AU, N_IA, IB_DEV, block_size, rank_width), -stratum, axis=1)
        accum_grid = jnp.roll(accum_new.reshape(N_AU, N_IA, IB_DEV, block_size, rank_width), -stratum, axis=1)
    return (user_grid.reshape(users.shape), item_grid.reshape(items.shape), accum_grid.reshape(accum.shape))
```

```python
import functools
import math

import jax
import jax.numpy as jnp
from jax import lax
from jax.experimental import pallas as pl
from jax.experimental.pallas import tpu as pltpu
from jax.sharding import PartitionSpec as P

STEPS = 2

rate_users = 0.1
rate_items = 0.1
weight_decay = 0.02
adagrad_eps = 1e-08

CHUNK = 256
F32 = jnp.float32
BF16 = jnp.bfloat16


def dot_nt(left, right):
    return lax.dot_general(left, right, (((1,), (1,)), ((), ())), preferred_element_type=F32)


def dot_nn(left, right):
    return lax.dot_general(left, right, (((1,), (0,)), ((), ())), preferred_element_type=F32)


def dot_tn(left, right):
    return lax.dot_general(left, right, (((0,), (0,)), ((), ())), preferred_element_type=F32)


def rating_copies(source, dense, ids_u, ids_i, row, stratum, sems, block):
    copies = []
    for n in range(source.shape[0]):
        user_at = pl.multiple_of(ids_u[row, 0, stratum, n] * block, block)
        item_at = pl.multiple_of(ids_i[row, 0, stratum, n] * block, block)
        copies.append(
            pltpu.make_async_copy(
                source.at[n], dense.at[pl.ds(user_at, block), pl.ds(item_at, block)], sems.at[n]
            )
        )
    return copies


def mark_live(live, ids_u, ids_i, counts, row, stratum, item_blocks):
    for at in range(live.shape[0]):
        live[at] = 0
    for n in range(ids_u.shape[-1]):
        @pl.when(n < counts[0, stratum, row])
        def _():
            live[ids_u[row, 0, stratum, n] * item_blocks + ids_i[row, 0, stratum, n]] = 1


def residual_chunk(predicted, dense, live, first, block, inv_root, out):
    rows, cols = predicted.shape
    item_blocks = cols // block
    for r in range(rows // block):
        for c in range(item_blocks):
            at = (pl.ds(first + r * block, block), pl.ds(c * block, block))
            part = predicted[r * block : (r + 1) * block, c * block : (c + 1) * block]
            flag = live[(first // block + r) * item_blocks + c] != 0
            value = jnp.where(flag, dense[at].astype(F32) - inv_root * part, 0.0)
            out[at] = value.astype(BF16)


def user_step(user, total, inv_root):
    return user - rate_users * (weight_decay * user - inv_root * total)


def item_step(item, acc, total, inv_root):
    grad = weight_decay * item - inv_root * total
    acc = acc + grad * grad
    return item - rate_items * grad / jnp.sqrt(acc + adagrad_eps), acc


def stratum_body(user, item, acc, dense, live, resid, item_total, user_out, copy_out, block):
    rows, width = user.shape
    inv_root = 1.0 / math.sqrt(width)
    for step in range(STEPS):
        last = step == STEPS - 1
        item_copy = item.astype(BF16)
        if last:
            copy_out[...] = item_copy
        source = user if step == 0 else user_out
        for c in range(rows // CHUNK):
            span = pl.ds(c * CHUNK, CHUNK)
            user_now = source[span, :]
            user_copy = user_now.astype(BF16)
            predicted = dot_nt(user_copy, item_copy)
            residual_chunk(predicted, dense, live, c * CHUNK, block, inv_root, resid)
            here = resid[span, :]
            part = dot_tn(here, user_copy)
            item_total[...] = part if c == 0 else item_total[...] + part
            if not last:
                user_out[span, :] = user_step(user_now, dot_nn(here, item_copy), inv_root)
        item, acc = item_step(item, acc, item_total[...], inv_root)
    return item, acc


def first_kernel(block, users, items, accum, ratings, ids_u, ids_i, counts,
                 user_out, resid, copy_out, item_out, acc_out, send_out,
                 dense, live, item_total, sems):
    row = lax.axis_index("au")
    copies = rating_copies(ratings.at[0, 0, 0], dense, ids_u, ids_i, row, 0, sems, block)
    for copy in copies:
        copy.start()
    mark_live(live, ids_u, ids_i, counts, row, 0, items.shape[0] // block)
    for copy in copies:
        copy.wait()
    item, acc = stratum_body(users, items[...], accum[...], dense, live, resid, item_total,
                             user_out, copy_out, block)
    item_out[...] = item
    acc_out[...] = acc
    send_out[0] = item.astype(BF16)
    send_out[1] = acc.astype(BF16)


def second_kernel(block, users, state, ratings, ids_u, ids_i, counts,
                  user_out, resid, copy_out, send_out,
                  dense, live, item_total, sems):
    row = lax.rem(lax.axis_index("au") + 1, lax.axis_size("au"))
    copies = rating_copies(ratings, dense, ids_u, ids_i, row, 1, sems, block)
    for copy in copies:
        copy.start()
    item_blocks = state.shape[1] // block
    mark_live(live, ids_u, ids_i, counts, row, 1, item_blocks)
    for copy in copies:
        copy.wait()
    item_first = state[0].astype(F32)
    acc_first = state[1].astype(F32)
    item, acc = stratum_body(users, item_first, acc_first, dense, live, resid, item_total,
                             user_out, copy_out, block)
    send_out[0] = (item - item_first).astype(BF16)
    send_out[1] = (acc - acc_first).astype(BF16)


def user_kernel(users, resid, item_copy, user_out):
    rows, width = users.shape
    inv_root = 1.0 / math.sqrt(width)
    for c in range(rows // CHUNK):
        span = pl.ds(c * CHUNK, CHUNK)
        total = dot_nn(resid[span, :], item_copy[...])
        user_out[span, :] = user_step(users[span, :], total, inv_root)


def vmem():
    return pl.BlockSpec(memory_space=pltpu.VMEM)


def smem():
    return pl.BlockSpec(memory_space=pltpu.SMEM)


def scratch(rows, cols, slots, live_count):
    return [
        pltpu.VMEM((rows, cols), BF16),
        pltpu.SMEM((live_count,), jnp.int32),
        pltpu.VMEM((cols, cols), F32),
        pltpu.SemaphoreType.DMA((slots,)),
    ]


def local(users, items, accum, ratings, block_users, block_items, block_counts):
    rows, width = users.shape
    cols = items.shape[0]
    slots, block = ratings.shape[3], ratings.shape[-1]
    live_count = (rows // block) * (cols // block)
    counts = jnp.transpose(block_counts, (1, 2, 0))
    n_au, n_ia = lax.axis_size("au"), lax.axis_size("ia")

    def at(a, i):
        return (a % n_au) * n_ia + i % n_ia

    places = [(a, i) for a in range(n_au) for i in range(n_ia)]
    out_pairs = [(at(a, i), at(a - 1, i + 1)) for a, i in places]
    back_pairs = [(target, source) for source, target in out_pairs]
    later = lax.ppermute(
        ratings[0, 0, 1], "au", [(a, (a - 1) % n_au) for a in range(n_au)]
    )
    shape = jax.ShapeDtypeStruct
    params = pltpu.CompilerParams(vmem_limit_bytes=24 << 20)
    user_mid, resid, item_copy, item_mid, acc_mid, sent = pl.pallas_call(
        functools.partial(first_kernel, block),
        out_shape=(
            shape((rows, width), F32),
            shape((rows, cols), BF16),
            shape((cols, width), BF16),
            shape((cols, width), F32),
            shape((cols, width), F32),
            shape((2, cols, width), BF16),
        ),
        in_specs=[vmem()] * 3 + [pl.BlockSpec(memory_space=pl.ANY)] + [smem()] * 3,
        out_specs=(vmem(),) * 6,
        scratch_shapes=scratch(rows, cols, slots, live_count),
        compiler_params=params,
    )(users, items, accum, ratings, block_users, block_items, counts)
    state = lax.ppermute(sent, ("au", "ia"), out_pairs)

    def finish(user_slab, residual, copy):
        return pl.pallas_call(
            user_kernel,
            out_shape=shape((rows, width), F32),
            in_specs=[vmem()] * 3,
            out_specs=vmem(),
            compiler_params=params,
        )(user_slab, residual, copy)

    user_mid = finish(user_mid, resid, item_copy)
    user_last, resid, item_copy, change = pl.pallas_call(
        functools.partial(second_kernel, block),
        out_shape=(
            shape((rows, width), F32),
            shape((rows, cols), BF16),
            shape((cols, width), BF16),
            shape((2, cols, width), BF16),
        ),
        in_specs=[vmem()] * 2 + [pl.BlockSpec(memory_space=pl.ANY)] + [smem()] * 3,
        out_specs=(vmem(),) * 4,
        scratch_shapes=scratch(rows, cols, slots, live_count),
        compiler_params=params,
    )(user_mid, state, later, block_users, block_items, counts)
    home = lax.ppermute(change, ("au", "ia"), back_pairs)
    user_last = finish(user_last, resid, item_copy)
    new_items = item_mid + home[0].astype(F32)
    new_accum = acc_mid + home[1].astype(F32)
    return user_last, new_items, new_accum


def solution(mesh):
    return jax.shard_map(
        local,
        mesh=mesh,
        in_specs=(
            P(("au", "ia"), None),
            P(("au", "ia"), None),
            P(("au", "ia"), None),
            P("au", "ia", None, None, None, None),
            P(None, "ia", None, None),
            P(None, "ia", None, None),
            P(None, "ia", None),
        ),
        out_specs=(P(("au", "ia"), None), P(("au", "ia"), None), P(("au", "ia"), None)),
        check_vma=False,
    )
```

```python
import functools
import math

import jax
import jax.numpy as jnp
from jax import lax
from jax.experimental import pallas as pl
from jax.experimental.pallas import tpu as pltpu
from jax.sharding import PartitionSpec as P

rate_users = 0.1
rate_items = 0.1
weight_decay = 0.02
adagrad_eps = 1e-08

CHUNK = 1024
F32 = jnp.float32
BF16 = jnp.bfloat16
TILE = 16


def dot(left, right, dims):
    return lax.dot_general(left, right, (dims, ((), ())), preferred_element_type=F32)


def rating_copies(source, dense, ids_u, ids_i, stratum, sems, block):
    copies = []
    for n in range(source.shape[0]):
        user_at = pl.multiple_of(ids_u[0, 0, stratum, n] * block, block)
        item_at = pl.multiple_of(ids_i[0, 0, stratum, n] * block, block)
        copies.append(
            pltpu.make_async_copy(
                source.at[n], dense.at[pl.ds(user_at, block), pl.ds(item_at, block)], sems.at[n]
            )
        )
    return copies


def fill_mask(mask, ids_u, ids_i, counts, stratum, row, item_blocks):
    mask[...] = jnp.zeros(mask.shape, BF16)
    for n in range(ids_u.shape[-1]):
        code = ids_u[0, 0, stratum, n] * item_blocks + ids_i[0, 0, stratum, n]
        live = jnp.where(n < counts[0, stratum, row], 1.0, 0.0)
        mask[code] = jnp.full(mask.shape[1:], live, F32).astype(BF16)


def id_copies(ids_u, ids_i, counts, ids_u_s, ids_i_s, counts_s, row, sems):
    here = pl.ds(row, 1)
    return [
        pltpu.make_async_copy(ids_u.at[here], ids_u_s, sems.at[0]),
        pltpu.make_async_copy(ids_i.at[here], ids_i_s, sems.at[1]),
        pltpu.make_async_copy(counts, counts_s, sems.at[2]),
    ]


def load_kernel(block, users, items, accum, ratings, ids_u, ids_i, counts,
                users_out, items_out, accum_out, later_out, dense, mask,
                ids_u_s, ids_i_s, counts_s, id_sems, data_sems, sems):
    row = lax.axis_index("au")
    small = id_copies(ids_u, ids_i, counts, ids_u_s, ids_i_s, counts_s, row, id_sems)
    large = [
        pltpu.make_async_copy(ratings.at[0, 0, 1], later_out, data_sems.at[0]),
        pltpu.make_async_copy(items, items_out, data_sems.at[1]),
        pltpu.make_async_copy(accum, accum_out, data_sems.at[2]),
        pltpu.make_async_copy(users, users_out, data_sems.at[3]),
    ]
    for copy in small + large:
        copy.start()
    for copy in small:
        copy.wait()
    slots = rating_copies(ratings.at[0, 0, 0], dense, ids_u_s, ids_i_s, 0, sems, block)
    for copy in slots:
        copy.start()
    fill_mask(mask, ids_u_s, ids_i_s, counts_s, 0, row, items.shape[0] // block)
    for copy in large + slots:
        copy.wait()


def residual_chunk(predicted, dense, mask, first, block, out):
    rows, cols = predicted.shape
    value = (dense[pl.ds(first, rows), :].astype(F32) - predicted).astype(BF16)
    for r in range(rows // block):
        for c in range(cols // block):
            part = value[r * block : (r + 1) * block, c * block : (c + 1) * block]
            flag = mask[(first // block + r) * (cols // block) + c]
            flag = jnp.concatenate([flag] * (block // TILE), axis=0)
            out[pl.ds(first + r * block, block), pl.ds(c * block, block)] = jnp.where(
                flag != 0, part, jnp.zeros_like(part)
            )


def sgd_step(source, scaled, dense, mask, resid, copies, user_out, block):
    rows = source.shape[0]
    for c in range(rows // CHUNK):
        span = pl.ds(c * CHUNK, CHUNK)
        user = source[span, :]
        user_copy = user.astype(BF16)
        copies[span, :] = user_copy
        predicted = dot(user_copy, scaled, ((1,), (1,)))
        residual_chunk(predicted, dense, mask, c * CHUNK, block, resid)
        if user_out is not None:
            user_out[span, :] = user_step(user, dot(resid[span, :], scaled, ((1,), (0,))))
    return dot(resid[...], copies[...], ((0,), (0,)))


def user_step(user, scaled_total):
    return (1.0 - rate_users * weight_decay) * user + rate_users * scaled_total


def item_step(item, acc, total):
    grad = weight_decay * item - (1.0 / math.sqrt(item.shape[-1])) * total
    acc = acc + grad * grad
    return item - rate_items * grad / jnp.sqrt(acc + adagrad_eps), acc


def scale(item):
    return item.astype(BF16) * BF16(1.0 / math.sqrt(item.shape[-1]))


def user_update(users, resid, scaled, user_out):
    for c in range(users.shape[0] // CHUNK):
        span = pl.ds(c * CHUNK, CHUNK)
        user_out[span, :] = user_step(users[span, :], dot(resid[span, :], scaled[...], ((1,), (0,))))


def first_kernel(block, users, items, accum, dense, mask,
                 user_out, resid, scaled_out, item_out, acc_out, item_send, acc_send, copies):
    item = items[...]
    total = sgd_step(users, scale(item), dense, mask, resid, copies, user_out, block)
    item, acc = item_step(item, accum[...], total)
    scaled = scale(item)
    scaled_out[...] = scaled
    total = sgd_step(user_out, scaled, dense, mask, resid, copies, None, block)
    item, acc = item_step(item, acc, total)
    item_out[...] = item
    acc_out[...] = acc
    item_send[...] = item.astype(BF16)
    acc_send[...] = acc.astype(BF16)


def turn_kernel(block, users, resid, scaled, later, ids_u, ids_i, counts, user_out, dense, mask,
                ids_u_s, ids_i_s, counts_s, id_sems, sems):
    row = lax.rem(lax.axis_index("au") + 1, lax.axis_size("au"))
    small = id_copies(ids_u, ids_i, counts, ids_u_s, ids_i_s, counts_s, row, id_sems)
    for copy in small:
        copy.start()
    for copy in small:
        copy.wait()
    slots = rating_copies(later, dense, ids_u_s, ids_i_s, 1, sems, block)
    for copy in slots:
        copy.start()
    fill_mask(mask, ids_u_s, ids_i_s, counts_s, 1, row, dense.shape[1] // block)
    user_update(users, resid, scaled, user_out)
    for copy in slots:
        copy.wait()


def second_kernel(block, users, items, dense, mask, user_out, total_out, resid, copies):
    scaled = scale(items[...].astype(F32))
    total_out[...] = sgd_step(users, scaled, dense, mask, resid, copies, user_out, block)


def third_kernel(block, users, items, accum, total, dense, mask,
                 resid, scaled_out, send, copies):
    item_first = items[...].astype(F32)
    acc_first = accum[...].astype(F32)
    item, acc = item_step(item_first, acc_first, total[...])
    scaled = scale(item)
    scaled_out[...] = scaled
    again = sgd_step(users, scaled, dense, mask, resid, copies, None, block)
    item, acc = item_step(item, acc, again)
    send[0] = (item - item_first).astype(BF16)
    send[1] = (acc - acc_first).astype(BF16)


def vmem(count):
    return [pl.BlockSpec(memory_space=pltpu.VMEM)] * count


def hbm(count):
    return [pl.BlockSpec(memory_space=pltpu.HBM)] * count


def call(body, in_specs, outs, scratch, args):
    return pl.pallas_call(
        body,
        out_shape=tuple(jax.ShapeDtypeStruct(shape, dtype) for shape, dtype in outs),
        in_specs=in_specs,
        out_specs=tuple(vmem(len(outs))),
        scratch_shapes=scratch,
        compiler_params=pltpu.CompilerParams(vmem_limit_bytes=24 << 20),
    )(*args)


def in_hbm(*values):
    return [pltpu.with_memory_space_constraint(value, pltpu.HBM) for value in values]


def local(users, items, accum, ratings, block_users, block_items, block_counts):
    rows, width = users.shape
    cols = items.shape[0]
    strata, slots, block = ratings.shape[2], ratings.shape[3], ratings.shape[-1]
    counts = jnp.transpose(block_counts, (1, 2, 0))
    n_au, n_ia = lax.axis_size("au"), lax.axis_size("ia")
    user_shape, item_shape = ((rows, width), F32), ((cols, width), F32)
    resid_shape, copy_shape = ((rows, cols), BF16), ((cols, width), BF16)
    slots_shape = ((slots, block, block), BF16)
    mask_shape = (((rows // block) * (cols // block), TILE, block), BF16)
    user_copies = pltpu.VMEM((rows, width), BF16)
    dma = pltpu.SemaphoreType.DMA
    ids_smem = pltpu.SMEM((1, 1, strata, slots), jnp.int32)

    def at(a, i):
        return (a % n_au) * n_ia + i % n_ia

    places = [(a, i) for a in range(n_au) for i in range(n_ia)]
    out_pairs = [(at(a, i), at(a - 1, i + 1)) for a, i in places]
    back_pairs = [(target, source) for source, target in out_pairs]

    tables = [ids_smem, ids_smem, pltpu.SMEM(counts.shape, jnp.int32), dma((3,))]
    user, item, acc, later, dense, mask = call(
        functools.partial(load_kernel, block),
        hbm(7),
        (user_shape, item_shape, item_shape, slots_shape, resid_shape, mask_shape),
        tables + [dma((4,)), dma((slots,))],
        in_hbm(users, items, accum, ratings, block_users, block_items, counts),
    )
    later = lax.ppermute(later, "au", [(a, (a - 1) % n_au) for a in range(n_au)])
    user, resid, scaled, item_mid, acc_mid, item_sent, acc_sent = call(
        functools.partial(first_kernel, block),
        vmem(5),
        (user_shape, resid_shape, copy_shape, item_shape, item_shape, copy_shape, copy_shape),
        [user_copies],
        (user, item, acc, dense, mask),
    )
    item_here = lax.ppermute(item_sent, ("au", "ia"), out_pairs)
    acc_here = lax.ppermute(acc_sent, ("au", "ia"), out_pairs)
    user, dense, mask = call(
        functools.partial(turn_kernel, block),
        vmem(4) + hbm(3),
        (user_shape, resid_shape, mask_shape),
        tables + [dma((slots,))],
        [user, resid, scaled, later] + in_hbm(block_users, block_items, counts),
    )
    user, total = call(
        functools.partial(second_kernel, block),
        vmem(4),
        (user_shape, item_shape),
        [pltpu.VMEM(*resid_shape), user_copies],
        (user, item_here, dense, mask),
    )
    resid, scaled, change = call(
        functools.partial(third_kernel, block),
        vmem(6),
        (resid_shape, copy_shape, ((2, cols, width), BF16)),
        [user_copies],
        (user, item_here, acc_here, total, dense, mask),
    )
    home = lax.ppermute(change, ("au", "ia"), back_pairs)
    (user,) = call(user_update, vmem(3), (user_shape,), [], (user, resid, scaled))
    return user, item_mid + home[0].astype(F32), acc_mid + home[1].astype(F32)


def solution(mesh):
    return jax.shard_map(
        local,
        mesh=mesh,
        in_specs=(
            P(("au", "ia"), None),
            P(("au", "ia"), None),
            P(("au", "ia"), None),
            P("au", "ia", None, None, None, None),
            P(None, "ia", None, None),
            P(None, "ia", None, None),
            P(None, "ia", None),
        ),
        out_specs=(P(("au", "ia"), None), P(("au", "ia"), None), P(("au", "ia"), None)),
        check_vma=False,
    )
```

```python
import functools
import math

import jax
import jax.numpy as jnp
from jax import lax
from jax.experimental import pallas as pl
from jax.experimental.pallas import tpu as pltpu
from jax.sharding import PartitionSpec as P


rate_users = 0.1
rate_items = 0.1
weight_decay = 0.02
adagrad_eps = 1e-08

CHUNK = 1024
F32 = jnp.float32
BF16 = jnp.bfloat16
TILE = 16
PIECES = 8


def dot(left, right, dims):
    return lax.dot_general(left, right, (dims, ((), ())), preferred_element_type=F32)


def place_slots(slots, dense, mask, ids_u, ids_i, counts, stratum, row, item_blocks):
    mask[...] = jnp.zeros(mask.shape, BF16)
    for n in range(slots.shape[0]):
        code = ids_u[0, 0, stratum, n] * item_blocks + ids_i[0, 0, stratum, n]
        live = jnp.where(n < counts[0, stratum, row], 1.0, 0.0)
        mask[code] = jnp.full(mask.shape[1:], live, F32).astype(BF16)
        dense[code] = slots[n]


def id_copies(ids_u, ids_i, counts, ids_u_s, ids_i_s, counts_s, row, sems):
    here = pl.ds(row, 1)
    return [
        pltpu.make_async_copy(ids_u.at[here], ids_u_s, sems.at[0]),
        pltpu.make_async_copy(ids_i.at[here], ids_i_s, sems.at[1]),
        pltpu.make_async_copy(counts, counts_s, sems.at[2]),
    ]


def load_kernel(block, users, items, accum, ratings, ids_u, ids_i, counts,
                users_out, items_out, accum_out, later_out, dense, mask,
                slots, ids_u_s, ids_i_s, counts_s, id_sems, data_sems):
    row = lax.axis_index("au")
    small = id_copies(ids_u, ids_i, counts, ids_u_s, ids_i_s, counts_s, row, id_sems)
    large = [
        pltpu.make_async_copy(ratings.at[0, 0, 0], slots, data_sems.at[0]),
        pltpu.make_async_copy(ratings.at[0, 0, 1], later_out, data_sems.at[1]),
        pltpu.make_async_copy(items, items_out, data_sems.at[2]),
        pltpu.make_async_copy(accum, accum_out, data_sems.at[3]),
    ]
    piece = users.shape[0] // PIECES
    for at in range(PIECES):
        span = pl.ds(at * piece, piece)
        large.append(
            pltpu.make_async_copy(users.at[span], users_out.at[span], data_sems.at[4 + at])
        )
    for copy in small + large:
        copy.start()
    for copy in small + large[:1]:
        copy.wait()
    place_slots(slots, dense, mask, ids_u_s, ids_i_s, counts_s, 0, row, items.shape[0] // block)
    for copy in large[1:]:
        copy.wait()


def residual_chunk(predicted, dense, mask, first, block, out):
    rows, cols = predicted.shape
    for r in range(rows // block):
        for c in range(cols // block):
            code = (first // block + r) * (cols // block) + c
            part = predicted[r * block : (r + 1) * block, c * block : (c + 1) * block]
            value = (dense[code].astype(F32) - part).astype(BF16)
            flag = jnp.concatenate([mask[code]] * (block // TILE), axis=0)
            out[pl.ds(first + r * block, block), pl.ds(c * block, block)] = jnp.where(
                flag != 0, value, jnp.zeros_like(value)
            )


def sgd_step(source, scaled, dense, mask, resid, copies, user_out, block):
    rows = source.shape[0]
    for c in range(rows // CHUNK):
        span = pl.ds(c * CHUNK, CHUNK)
        user = source[span, :]
        user_copy = user.astype(BF16)
        copies[span, :] = user_copy
        predicted = dot(user_copy, scaled, ((1,), (1,)))
        residual_chunk(predicted, dense, mask, c * CHUNK, block, resid)
        if user_out is not None:
            user_out[span, :] = user_step(user, dot(resid[span, :], scaled, ((1,), (0,))))
    return dot(resid[...], copies[...], ((0,), (0,)))


def user_step(user, scaled_total):
    return (1.0 - rate_users * weight_decay) * user + rate_users * scaled_total


def adagrad(item, acc, grad):
    acc = acc + grad * grad
    return item - rate_items * grad / jnp.sqrt(acc + adagrad_eps), acc


def item_step(item, acc, total):
    return adagrad(item, acc, gradient(item, total))


def scale(item):
    return item.astype(BF16) * BF16(1.0 / math.sqrt(item.shape[-1]))


def user_update(users, resid, scaled, user_out):
    for c in range(users.shape[0] // CHUNK):
        span = pl.ds(c * CHUNK, CHUNK)
        user_out[span, :] = user_step(users[span, :], dot(resid[span, :], scaled[...], ((1,), (0,))))


def first_kernel(block, users, items, accum, dense, mask,
                 user_out, resid, scaled_out, item_out, acc_out, item_send, acc_send, copies):
    item = items[...]
    total = sgd_step(users, scale(item), dense, mask, resid, copies, user_out, block)
    item, acc = item_step(item, accum[...], total)
    scaled = scale(item)
    scaled_out[...] = scaled
    total = sgd_step(user_out, scaled, dense, mask, resid, copies, None, block)
    item, acc = item_step(item, acc, total)
    item_out[...] = item
    acc_out[...] = acc
    item_send[...] = item.astype(BF16)
    acc_send[...] = acc.astype(BF16)


def turn_kernel(item_blocks, users, resid, scaled, later, ids_u, ids_i, counts,
                user_out, dense, mask, ids_u_s, ids_i_s, counts_s, id_sems):
    row = lax.rem(lax.axis_index("au") + 1, lax.axis_size("au"))
    small = id_copies(ids_u, ids_i, counts, ids_u_s, ids_i_s, counts_s, row, id_sems)
    for copy in small:
        copy.start()
    user_update(users, resid, scaled, user_out)
    for copy in small:
        copy.wait()
    place_slots(later, dense, mask, ids_u_s, ids_i_s, counts_s, 1, row, item_blocks)


def gradient(item, total):
    return weight_decay * item - (1.0 / math.sqrt(item.shape[-1])) * total


def second_kernel(block, users, items, dense, mask, user_out, grad_out, grad_send, resid, copies):
    item = items[...].astype(F32)
    total = sgd_step(users, scale(item), dense, mask, resid, copies, user_out, block)
    grad = gradient(item, total)
    grad_out[...] = grad
    grad_send[...] = grad.astype(BF16)


def third_kernel(block, users, items, accum, grad, dense, mask,
                 resid, scaled_out, grad_send, copies):
    item, _ = adagrad(items[...].astype(F32), accum[...].astype(F32), grad[...])
    scaled = scale(item)
    scaled_out[...] = scaled
    total = sgd_step(users, scaled, dense, mask, resid, copies, None, block)
    grad_send[...] = gradient(item, total).astype(BF16)


def vmem(count):
    return [pl.BlockSpec(memory_space=pltpu.VMEM)] * count


def hbm(count):
    return [pl.BlockSpec(memory_space=pltpu.HBM)] * count


def call(body, in_specs, outs, scratch, args):
    return pl.pallas_call(
        body,
        out_shape=tuple(jax.ShapeDtypeStruct(shape, dtype) for shape, dtype in outs),
        in_specs=in_specs,
        out_specs=tuple(vmem(len(outs))),
        scratch_shapes=scratch,
        compiler_params=pltpu.CompilerParams(vmem_limit_bytes=24 << 20),
    )(*args)


def in_hbm(*values):
    return [pltpu.with_memory_space_constraint(value, pltpu.HBM) for value in values]


def whole(users, items, accum, ratings, block_users, block_items, block_counts):
    rows, width = users.shape
    cols = items.shape[0]
    strata, slots, block = ratings.shape[2], ratings.shape[3], ratings.shape[-1]
    counts = jnp.transpose(block_counts, (1, 2, 0))
    n_au, n_ia = lax.axis_size("au"), lax.axis_size("ia")
    user_shape, item_shape = ((rows, width), F32), ((cols, width), F32)
    resid_shape, copy_shape = ((rows, cols), BF16), ((cols, width), BF16)
    slots_shape = ((slots, block, block), BF16)
    dense_shape = (((rows // block) * (cols // block), block, block), BF16)
    mask_shape = (((rows // block) * (cols // block), TILE, block), BF16)
    user_copies = pltpu.VMEM((rows, width), BF16)
    dma = pltpu.SemaphoreType.DMA
    ids_smem = pltpu.SMEM((1, 1, strata, slots), jnp.int32)

    def at(a, i):
        return (a % n_au) * n_ia + i % n_ia

    places = [(a, i) for a in range(n_au) for i in range(n_ia)]
    out_pairs = [(at(a, i), at(a - 1, i + 1)) for a, i in places]
    back_pairs = [(target, source) for source, target in out_pairs]

    tables = [ids_smem, ids_smem, pltpu.SMEM(counts.shape, jnp.int32), dma((3,))]
    user, item, acc, later, dense, mask = call(
        functools.partial(load_kernel, block),
        hbm(7),
        (user_shape, item_shape, item_shape, slots_shape, dense_shape, mask_shape),
        [pltpu.VMEM(*slots_shape)] + tables + [dma((4 + PIECES,))],
        in_hbm(users, items, accum, ratings, block_users, block_items, counts),
    )
    later = lax.ppermute(later, "au", [(a, (a - 1) % n_au) for a in range(n_au)])
    user, resid, scaled, item_mid, acc_mid, item_sent, acc_sent = call(
        functools.partial(first_kernel, block),
        vmem(5),
        (user_shape, resid_shape, copy_shape, item_shape, item_shape, copy_shape, copy_shape),
        [user_copies],
        (user, item, acc, dense, mask),
    )
    item_here = lax.ppermute(item_sent, ("au", "ia"), out_pairs)
    acc_here = lax.ppermute(acc_sent, ("au", "ia"), out_pairs)
    user, dense, mask = call(
        functools.partial(turn_kernel, cols // block),
        vmem(4) + hbm(3),
        (user_shape, dense_shape, mask_shape),
        tables,
        [user, resid, scaled, later] + in_hbm(block_users, block_items, counts),
    )
    user, grad, grad_sent = call(
        functools.partial(second_kernel, block),
        vmem(4),
        (user_shape, item_shape, copy_shape),
        [pltpu.VMEM(*resid_shape), user_copies],
        (user, item_here, dense, mask),
    )
    home = lax.ppermute(grad_sent, ("au", "ia"), back_pairs)
    resid, scaled, grad_sent = call(
        functools.partial(third_kernel, block),
        vmem(6),
        (resid_shape, copy_shape, copy_shape),
        [user_copies],
        (user, item_here, acc_here, grad, dense, mask),
    )
    home_last = lax.ppermute(grad_sent, ("au", "ia"), back_pairs)
    (user,) = call(user_update, vmem(3), (user_shape,), [], (user, resid, scaled))
    new_items, new_accum = adagrad(item_mid, acc_mid, home.astype(F32))
    new_items, new_accum = adagrad(new_items, new_accum, home_last.astype(F32))
    return user, new_items, new_accum


def solution(mesh):
    return jax.shard_map(
        whole,
        mesh=mesh,
        in_specs=(
            P(("au", "ia"), None),
            P(("au", "ia"), None),
            P(("au", "ia"), None),
            P("au", "ia", None, None, None, None),
            P(None, "ia", None, None),
            P(None, "ia", None, None),
            P(None, "ia", None),
        ),
        out_specs=(P(("au", "ia"), None), P(("au", "ia"), None), P(("au", "ia"), None)),
        check_vma=False,
    )
```

```python
import functools
import math

import jax
import jax.numpy as jnp
from jax import lax
from jax.experimental import pallas as pl
from jax.experimental.pallas import tpu as pltpu
from jax.sharding import PartitionSpec as P


rate_users = 0.1
rate_items = 0.1
weight_decay = 0.02
adagrad_eps = 1e-08

CHUNK = 1024
F32 = jnp.float32
BF16 = jnp.bfloat16
TILE = 16
PIECES = 8


def dot(left, right, dims):
    return lax.dot_general(left, right, (dims, ((), ())), preferred_element_type=F32)


def place_slots(slots, dense, mask, ids_u, ids_i, counts, stratum, row, item_blocks):
    mask[...] = jnp.zeros(mask.shape, BF16)
    for n in range(slots.shape[0]):
        code = ids_u[0, 0, stratum, n] * item_blocks + ids_i[0, 0, stratum, n]
        live = jnp.where(n < counts[0, stratum, row], 1.0, 0.0)
        mask[code] = jnp.full(mask.shape[1:], live, F32).astype(BF16)
        dense[code] = slots[n]


def id_copies(ids_u, ids_i, counts, ids_u_s, ids_i_s, counts_s, row, sems):
    here = pl.ds(row, 1)
    return [
        pltpu.make_async_copy(ids_u.at[here], ids_u_s, sems.at[0]),
        pltpu.make_async_copy(ids_i.at[here], ids_i_s, sems.at[1]),
        pltpu.make_async_copy(counts, counts_s, sems.at[2]),
    ]


def load_kernel(block, users, items, accum, ratings, ids_u, ids_i, counts,
                users_out, items_out, accum_out, later_out, dense, mask,
                slots, ids_u_s, ids_i_s, counts_s, id_sems, data_sems):
    row = lax.axis_index("au")
    small = id_copies(ids_u, ids_i, counts, ids_u_s, ids_i_s, counts_s, row, id_sems)
    large = [
        pltpu.make_async_copy(ratings.at[0, 0, 0], slots, data_sems.at[0]),
        pltpu.make_async_copy(ratings.at[0, 0, 1], later_out, data_sems.at[1]),
        pltpu.make_async_copy(items, items_out, data_sems.at[2]),
        pltpu.make_async_copy(accum, accum_out, data_sems.at[3]),
    ]
    piece = users.shape[0] // PIECES
    for at in range(PIECES):
        span = pl.ds(at * piece, piece)
        large.append(
            pltpu.make_async_copy(users.at[span], users_out.at[span], data_sems.at[4 + at])
        )
    for copy in small + large:
        copy.start()
    for copy in small + large[:1]:
        copy.wait()
    place_slots(slots, dense, mask, ids_u_s, ids_i_s, counts_s, 0, row, items.shape[0] // block)
    for copy in large[1:]:
        copy.wait()


def residual_chunk(predicted, dense, mask, first, block, out):
    rows, cols = predicted.shape
    for r in range(rows // block):
        for c in range(cols // block):
            code = (first // block + r) * (cols // block) + c
            part = predicted[r * block : (r + 1) * block, c * block : (c + 1) * block]
            value = (dense[code].astype(F32) - part).astype(BF16)
            flag = jnp.concatenate([mask[code]] * (block // TILE), axis=0)
            out[pl.ds(first + r * block, block), pl.ds(c * block, block)] = jnp.where(
                flag != 0, value, jnp.zeros_like(value)
            )


def sgd_step(source, scaled, dense, mask, resid, copies, user_out, block):
    rows = source.shape[0]
    for c in range(rows // CHUNK):
        span = pl.ds(c * CHUNK, CHUNK)
        user = source[span, :]
        user_copy = user.astype(BF16)
        copies[span, :] = user_copy
        predicted = dot(user_copy, scaled, ((1,), (1,)))
        residual_chunk(predicted, dense, mask, c * CHUNK, block, resid)
        if user_out is not None:
            user_out[span, :] = user_step(user, dot(resid[span, :], scaled, ((1,), (0,))))
    return dot(resid[...], copies[...], ((0,), (0,)))


def user_step(user, scaled_total):
    return (1.0 - rate_users * weight_decay) * user + rate_users * scaled_total


def adagrad(item, acc, grad):
    acc = acc + grad * grad
    return item - rate_items * grad / jnp.sqrt(acc + adagrad_eps), acc


def item_step(item, acc, total):
    return adagrad(item, acc, gradient(item, total))


def scale(item):
    return item.astype(BF16) * BF16(1.0 / math.sqrt(item.shape[-1]))


def user_update(users, resid, scaled, user_out):
    for c in range(users.shape[0] // CHUNK):
        span = pl.ds(c * CHUNK, CHUNK)
        user_out[span, :] = user_step(users[span, :], dot(resid[span, :], scaled[...], ((1,), (0,))))


def first_kernel(block, users, items, accum, dense, mask,
                 user_out, resid, scaled_out, item_out, acc_out, item_send, acc_send, copies):
    item = items[...]
    total = sgd_step(users, scale(item), dense, mask, resid, copies, user_out, block)
    item, acc = item_step(item, accum[...], total)
    scaled = scale(item)
    scaled_out[...] = scaled
    total = sgd_step(user_out, scaled, dense, mask, resid, copies, None, block)
    item, acc = item_step(item, acc, total)
    item_out[...] = item
    acc_out[...] = acc
    item_send[...] = item.astype(BF16)
    acc_send[...] = acc.astype(BF16)


def turn_kernel(item_blocks, users, resid, scaled, ids_u, ids_i, counts,
                user_out, mask, codes, ids_u_s, ids_i_s, counts_s, id_sems):
    row = lax.rem(lax.axis_index("au") + 1, lax.axis_size("au"))
    small = id_copies(ids_u, ids_i, counts, ids_u_s, ids_i_s, counts_s, row, id_sems)
    for copy in small:
        copy.start()
    user_update(users, resid, scaled, user_out)
    for copy in small:
        copy.wait()
    mask[...] = jnp.zeros(mask.shape, BF16)
    for n in range(codes.shape[0]):
        code = ids_u_s[0, 0, 1, n] * item_blocks + ids_i_s[0, 0, 1, n]
        live = jnp.where(n < counts_s[0, 1, row], 1.0, 0.0)
        mask[code] = jnp.full(mask.shape[1:], live, F32).astype(BF16)
        codes[n] = code


def place_kernel(later, codes, dense):
    for n in range(later.shape[0]):
        dense[codes[n]] = later[n]


def gradient(item, total):
    return weight_decay * item - (1.0 / math.sqrt(item.shape[-1])) * total


def second_kernel(block, users, items, dense, mask, user_out, grad_out, grad_send, resid, copies):
    item = items[...].astype(F32)
    total = sgd_step(users, scale(item), dense, mask, resid, copies, user_out, block)
    grad = gradient(item, total)
    grad_out[...] = grad
    grad_send[...] = grad.astype(BF16)


def third_kernel(block, users, items, accum, grad, dense, mask,
                 resid, scaled_out, grad_send, copies):
    item, _ = adagrad(items[...].astype(F32), accum[...].astype(F32), grad[...])
    scaled = scale(item)
    scaled_out[...] = scaled
    total = sgd_step(users, scaled, dense, mask, resid, copies, None, block)
    grad_send[...] = gradient(item, total).astype(BF16)


def vmem(count):
    return [pl.BlockSpec(memory_space=pltpu.VMEM)] * count


def hbm(count):
    return [pl.BlockSpec(memory_space=pltpu.HBM)] * count


def call(body, in_specs, outs, scratch, args, out_specs=None):
    return pl.pallas_call(
        body,
        out_shape=tuple(jax.ShapeDtypeStruct(shape, dtype) for shape, dtype in outs),
        in_specs=in_specs,
        out_specs=tuple(out_specs or vmem(len(outs))),
        scratch_shapes=scratch,
        compiler_params=pltpu.CompilerParams(vmem_limit_bytes=24 << 20),
    )(*args)


def in_hbm(*values):
    return [pltpu.with_memory_space_constraint(value, pltpu.HBM) for value in values]


def whole(users, items, accum, ratings, block_users, block_items, block_counts):
    rows, width = users.shape
    cols = items.shape[0]
    strata, slots, block = ratings.shape[2], ratings.shape[3], ratings.shape[-1]
    counts = jnp.transpose(block_counts, (1, 2, 0))
    n_au, n_ia = lax.axis_size("au"), lax.axis_size("ia")
    user_shape, item_shape = ((rows, width), F32), ((cols, width), F32)
    resid_shape, copy_shape = ((rows, cols), BF16), ((cols, width), BF16)
    slots_shape = ((slots, block, block), BF16)
    dense_shape = (((rows // block) * (cols // block), block, block), BF16)
    mask_shape = (((rows // block) * (cols // block), TILE, block), BF16)
    user_copies = pltpu.VMEM((rows, width), BF16)
    dma = pltpu.SemaphoreType.DMA
    ids_smem = pltpu.SMEM((1, 1, strata, slots), jnp.int32)

    def at(a, i):
        return (a % n_au) * n_ia + i % n_ia

    places = [(a, i) for a in range(n_au) for i in range(n_ia)]
    out_pairs = [(at(a, i), at(a - 1, i + 1)) for a, i in places]
    back_pairs = [(target, source) for source, target in out_pairs]

    tables = [ids_smem, ids_smem, pltpu.SMEM(counts.shape, jnp.int32), dma((3,))]
    user, item, acc, later, dense, mask = call(
        functools.partial(load_kernel, block),
        hbm(7),
        (user_shape, item_shape, item_shape, slots_shape, dense_shape, mask_shape),
        [pltpu.VMEM(*slots_shape)] + tables + [dma((4 + PIECES,))],
        in_hbm(users, items, accum, ratings, block_users, block_items, counts),
    )
    later = lax.ppermute(later, "au", [(a, (a - 1) % n_au) for a in range(n_au)])
    user, resid, scaled, item_mid, acc_mid, item_sent, acc_sent = call(
        functools.partial(first_kernel, block),
        vmem(5),
        (user_shape, resid_shape, copy_shape, item_shape, item_shape, copy_shape, copy_shape),
        [user_copies],
        (user, item, acc, dense, mask),
    )
    item_here = lax.ppermute(item_sent, ("au", "ia"), out_pairs)
    acc_here = lax.ppermute(acc_sent, ("au", "ia"), out_pairs)
    smem = [pl.BlockSpec(memory_space=pltpu.SMEM)]
    user, mask, codes = call(
        functools.partial(turn_kernel, cols // block),
        vmem(3) + hbm(3),
        (user_shape, mask_shape, ((slots,), jnp.int32)),
        tables,
        [user, resid, scaled] + in_hbm(block_users, block_items, counts),
        vmem(2) + smem,
    )
    (dense,) = call(place_kernel, vmem(1) + smem, (dense_shape,), [], (later, codes))
    user, grad, grad_sent = call(
        functools.partial(second_kernel, block),
        vmem(4),
        (user_shape, item_shape, copy_shape),
        [pltpu.VMEM(*resid_shape), user_copies],
        (user, item_here, dense, mask),
    )
    home = lax.ppermute(grad_sent, ("au", "ia"), back_pairs)
    resid, scaled, grad_sent = call(
        functools.partial(third_kernel, block),
        vmem(6),
        (resid_shape, copy_shape, copy_shape),
        [user_copies],
        (user, item_here, acc_here, grad, dense, mask),
    )
    home_last = lax.ppermute(grad_sent, ("au", "ia"), back_pairs)
    (user,) = call(user_update, vmem(3), (user_shape,), [], (user, resid, scaled))
    new_items, new_accum = adagrad(item_mid, acc_mid, home.astype(F32))
    new_items, new_accum = adagrad(new_items, new_accum, home_last.astype(F32))
    return user, new_items, new_accum


def solution(mesh):
    return jax.shard_map(
        whole,
        mesh=mesh,
        in_specs=(
            P(("au", "ia"), None),
            P(("au", "ia"), None),
            P(("au", "ia"), None),
            P("au", "ia", None, None, None, None),
            P(None, "ia", None, None),
            P(None, "ia", None, None),
            P(None, "ia", None),
        ),
        out_specs=(P(("au", "ia"), None), P(("au", "ia"), None), P(("au", "ia"), None)),
        check_vma=False,
    )
```

```python
import functools
import math

import jax
import jax.numpy as jnp
from jax import lax
from jax.experimental import pallas as pl
from jax.experimental.pallas import tpu as pltpu
from jax.sharding import PartitionSpec as P


rate_users = 0.1
rate_items = 0.1
weight_decay = 0.02
adagrad_eps = 1e-08

CHUNK = 1024
F32 = jnp.float32
BF16 = jnp.bfloat16
TILE = 16
PIECES = 8


def dot(left, right, dims):
    return lax.dot_general(left, right, (dims, ((), ())), preferred_element_type=F32)


def place_slots(slots, dense, mask, ids_u, ids_i, counts, stratum, row, item_blocks):
    mask[...] = jnp.zeros(mask.shape, BF16)
    for n in range(slots.shape[0]):
        code = ids_u[0, 0, stratum, n] * item_blocks + ids_i[0, 0, stratum, n]
        live = jnp.where(n < counts[0, stratum, row], 1.0, 0.0)
        mask[code] = jnp.full(mask.shape[1:], live, F32).astype(BF16)
        dense[code] = slots[n]


def id_copies(ids_u, ids_i, counts, ids_u_s, ids_i_s, counts_s, row, sems):
    here = pl.ds(row, 1)
    return [
        pltpu.make_async_copy(ids_u.at[here], ids_u_s, sems.at[0]),
        pltpu.make_async_copy(ids_i.at[here], ids_i_s, sems.at[1]),
        pltpu.make_async_copy(counts, counts_s, sems.at[2]),
    ]


def load_kernel(block, users, items, accum, ratings, ids_u, ids_i, counts,
                users_out, items_out, accum_out, later_out, dense, mask,
                slots, ids_u_s, ids_i_s, counts_s, id_sems, data_sems):
    row = lax.axis_index("au")
    small = id_copies(ids_u, ids_i, counts, ids_u_s, ids_i_s, counts_s, row, id_sems)
    large = [
        pltpu.make_async_copy(ratings.at[0, 0, 0], slots, data_sems.at[0]),
        pltpu.make_async_copy(ratings.at[0, 0, 1], later_out, data_sems.at[1]),
        pltpu.make_async_copy(items, items_out, data_sems.at[2]),
        pltpu.make_async_copy(accum, accum_out, data_sems.at[3]),
    ]
    piece = users.shape[0] // PIECES
    for at in range(PIECES):
        span = pl.ds(at * piece, piece)
        large.append(
            pltpu.make_async_copy(users.at[span], users_out.at[span], data_sems.at[4 + at])
        )
    for copy in small + large:
        copy.start()
    for copy in small + large[:1]:
        copy.wait()
    place_slots(slots, dense, mask, ids_u_s, ids_i_s, counts_s, 0, row, items.shape[0] // block)
    for copy in large[1:]:
        copy.wait()


def residual_chunk(predicted, dense, mask, first, block):
    rows, cols = predicted.shape

    def spread(piece):
        item_blocks = cols // block
        return jnp.concatenate(
            [
                jnp.concatenate(
                    [piece((first // block + r) * item_blocks + c) for c in range(item_blocks)],
                    axis=1,
                )
                for r in range(rows // block)
            ],
            axis=0,
        )

    value = (spread(lambda code: dense[code]).astype(F32) - predicted).astype(BF16)
    live = spread(lambda code: jnp.concatenate([mask[code]] * (block // TILE), axis=0))
    return jnp.where(live != 0, value, jnp.zeros_like(value))


def sgd_step(source, scaled, dense, mask, resid, copies, user_out, block):
    rows = source.shape[0]
    for c in range(rows // CHUNK):
        span = pl.ds(c * CHUNK, CHUNK)
        user = source[span, :]
        user_copy = user.astype(BF16)
        copies[span, :] = user_copy
        predicted = dot(user_copy, scaled, ((1,), (1,)))
        here = residual_chunk(predicted, dense, mask, c * CHUNK, block)
        resid[span, :] = here
        if user_out is not None:
            user_out[span, :] = user_step(user, dot(here, scaled, ((1,), (0,))))
    return dot(resid[...], copies[...], ((0,), (0,)))


def user_step(user, scaled_total):
    return (1.0 - rate_users * weight_decay) * user + rate_users * scaled_total


def adagrad(item, acc, grad):
    acc = acc + grad * grad
    return item - rate_items * grad / jnp.sqrt(acc + adagrad_eps), acc


def item_step(item, acc, total):
    return adagrad(item, acc, gradient(item, total))


def scale(item):
    return item.astype(BF16) * BF16(1.0 / math.sqrt(item.shape[-1]))


def user_update(users, resid, scaled, user_out):
    for c in range(users.shape[0] // CHUNK):
        span = pl.ds(c * CHUNK, CHUNK)
        user_out[span, :] = user_step(users[span, :], dot(resid[span, :], scaled[...], ((1,), (0,))))


def first_kernel(block, users, items, accum, dense, mask,
                 user_out, resid, scaled_out, item_out, acc_out, item_send, acc_send, copies):
    item = items[...]
    total = sgd_step(users, scale(item), dense, mask, resid, copies, user_out, block)
    item, acc = item_step(item, accum[...], total)
    scaled = scale(item)
    scaled_out[...] = scaled
    total = sgd_step(user_out, scaled, dense, mask, resid, copies, None, block)
    item, acc = item_step(item, acc, total)
    item_out[...] = item
    acc_out[...] = acc
    item_send[...] = item.astype(BF16)
    acc_send[...] = acc.astype(BF16)


def turn_kernel(item_blocks, users, resid, scaled, ids_u, ids_i, counts,
                user_out, mask, codes, ids_u_s, ids_i_s, counts_s, id_sems):
    row = lax.rem(lax.axis_index("au") + 1, lax.axis_size("au"))
    small = id_copies(ids_u, ids_i, counts, ids_u_s, ids_i_s, counts_s, row, id_sems)
    for copy in small:
        copy.start()
    user_update(users, resid, scaled, user_out)
    for copy in small:
        copy.wait()
    mask[...] = jnp.zeros(mask.shape, BF16)
    for n in range(codes.shape[0]):
        code = ids_u_s[0, 0, 1, n] * item_blocks + ids_i_s[0, 0, 1, n]
        live = jnp.where(n < counts_s[0, 1, row], 1.0, 0.0)
        mask[code] = jnp.full(mask.shape[1:], live, F32).astype(BF16)
        codes[n] = code


def place_kernel(later, codes, dense):
    for n in range(later.shape[0]):
        dense[codes[n]] = later[n]


def gradient(item, total):
    return weight_decay * item - (1.0 / math.sqrt(item.shape[-1])) * total


def second_kernel(block, users, items, dense, mask, user_out, grad_out, grad_send, resid, copies):
    item = items[...].astype(F32)
    total = sgd_step(users, scale(item), dense, mask, resid, copies, user_out, block)
    grad = gradient(item, total)
    grad_out[...] = grad
    grad_send[...] = grad.astype(BF16)


def third_kernel(block, users, items, accum, grad, dense, mask,
                 resid, scaled_out, grad_send, copies):
    item, _ = adagrad(items[...].astype(F32), accum[...].astype(F32), grad[...])
    scaled = scale(item)
    scaled_out[...] = scaled
    total = sgd_step(users, scaled, dense, mask, resid, copies, None, block)
    grad_send[...] = gradient(item, total).astype(BF16)


def vmem(count):
    return [pl.BlockSpec(memory_space=pltpu.VMEM)] * count


def hbm(count):
    return [pl.BlockSpec(memory_space=pltpu.HBM)] * count


def call(body, in_specs, outs, scratch, args, out_specs=None):
    return pl.pallas_call(
        body,
        out_shape=tuple(jax.ShapeDtypeStruct(shape, dtype) for shape, dtype in outs),
        in_specs=in_specs,
        out_specs=tuple(out_specs or vmem(len(outs))),
        scratch_shapes=scratch,
        compiler_params=pltpu.CompilerParams(vmem_limit_bytes=24 << 20),
    )(*args)


def in_hbm(*values):
    return [pltpu.with_memory_space_constraint(value, pltpu.HBM) for value in values]


def whole(users, items, accum, ratings, block_users, block_items, block_counts):
    rows, width = users.shape
    cols = items.shape[0]
    strata, slots, block = ratings.shape[2], ratings.shape[3], ratings.shape[-1]
    counts = jnp.transpose(block_counts, (1, 2, 0))
    n_au, n_ia = lax.axis_size("au"), lax.axis_size("ia")
    user_shape, item_shape = ((rows, width), F32), ((cols, width), F32)
    resid_shape, copy_shape = ((rows, cols), BF16), ((cols, width), BF16)
    slots_shape = ((slots, block, block), BF16)
    dense_shape = (((rows // block) * (cols // block), block, block), BF16)
    mask_shape = (((rows // block) * (cols // block), TILE, block), BF16)
    user_copies = pltpu.VMEM((rows, width), BF16)
    dma = pltpu.SemaphoreType.DMA
    ids_smem = pltpu.SMEM((1, 1, strata, slots), jnp.int32)

    def at(a, i):
        return (a % n_au) * n_ia + i % n_ia

    places = [(a, i) for a in range(n_au) for i in range(n_ia)]
    out_pairs = [(at(a, i), at(a - 1, i + 1)) for a, i in places]
    back_pairs = [(target, source) for source, target in out_pairs]

    tables = [ids_smem, ids_smem, pltpu.SMEM(counts.shape, jnp.int32), dma((3,))]
    user, item, acc, later, dense, mask = call(
        functools.partial(load_kernel, block),
        hbm(7),
        (user_shape, item_shape, item_shape, slots_shape, dense_shape, mask_shape),
        [pltpu.VMEM(*slots_shape)] + tables + [dma((4 + PIECES,))],
        in_hbm(users, items, accum, ratings, block_users, block_items, counts),
    )
    later = lax.ppermute(later, "au", [(a, (a - 1) % n_au) for a in range(n_au)])
    user, resid, scaled, item_mid, acc_mid, item_sent, acc_sent = call(
        functools.partial(first_kernel, block),
        vmem(5),
        (user_shape, resid_shape, copy_shape, item_shape, item_shape, copy_shape, copy_shape),
        [user_copies],
        (user, item, acc, dense, mask),
    )
    item_here = lax.ppermute(item_sent, ("au", "ia"), out_pairs)
    acc_here = lax.ppermute(acc_sent, ("au", "ia"), out_pairs)
    smem = [pl.BlockSpec(memory_space=pltpu.SMEM)]
    user, mask, codes = call(
        functools.partial(turn_kernel, cols // block),
        vmem(3) + hbm(3),
        (user_shape, mask_shape, ((slots,), jnp.int32)),
        tables,
        [user, resid, scaled] + in_hbm(block_users, block_items, counts),
        vmem(2) + smem,
    )
    (dense,) = call(place_kernel, vmem(1) + smem, (dense_shape,), [], (later, codes))
    user, grad, grad_sent = call(
        functools.partial(second_kernel, block),
        vmem(4),
        (user_shape, item_shape, copy_shape),
        [pltpu.VMEM(*resid_shape), user_copies],
        (user, item_here, dense, mask),
    )
    home = lax.ppermute(grad_sent, ("au", "ia"), back_pairs)
    resid, scaled, grad_sent = call(
        functools.partial(third_kernel, block),
        vmem(6),
        (resid_shape, copy_shape, copy_shape),
        [user_copies],
        (user, item_here, acc_here, grad, dense, mask),
    )
    home_last = lax.ppermute(grad_sent, ("au", "ia"), back_pairs)
    (user,) = call(user_update, vmem(3), (user_shape,), [], (user, resid, scaled))
    new_items, new_accum = adagrad(item_mid, acc_mid, home.astype(F32))
    new_items, new_accum = adagrad(new_items, new_accum, home_last.astype(F32))
    return user, new_items, new_accum


def solution(mesh):
    return jax.shard_map(
        whole,
        mesh=mesh,
        in_specs=(
            P(("au", "ia"), None),
            P(("au", "ia"), None),
            P(("au", "ia"), None),
            P("au", "ia", None, None, None, None),
            P(None, "ia", None, None),
            P(None, "ia", None, None),
            P(None, "ia", None),
        ),
        out_specs=(P(("au", "ia"), None), P(("au", "ia"), None), P(("au", "ia"), None)),
        check_vma=False,
    )
```
